256 devices in a mesh: wide: 32 (over y, x, core), grp: 8 (over z).
Axes of the slice: x: 4, y: 4, z: 8, core: 2. Of those that a mesh axis runs over, the one named last changes fastest.
Arguments:
- solution: float32 [64, 262144], P(None, ('wide', 'grp')), may hold values from -6 to 6
- incident: float32 [64, 262144], P(None, ('wide', 'grp')), may hold values from -12 to 12
- leaf_blocks: float32 [512, 262144], P(None, ('wide', 'grp')), may hold values from -0.25 to 0.25
- leaf_inverse: float32 [512, 262144], P(None, ('wide', 'grp')), may hold values from -0.25 to 0.25
- col_basis: float32 [9, 96, 262144], P(None, None, ('wide', 'grp')), may hold values from -0.625 to 0.625
- row_basis: float32 [9, 96, 262144], P(None, None, ('wide', 'grp')), may hold values from -6 to 6
Outputs:
- refined: float32 [64, 262144], P(None, ('wide', 'grp'))
- residual: float32 [64, 262144], P(None, ('wide', 'grp'))
The draws below stay inside these ranges and needn't reach their ends.
All inputs are finite; a program needn't handle non-finite values.
Results may differ from the reference program's by a relative error of at most 0.0001.
Values sent between devices are 32-bit elements; how exact they have to be, the bound alone decides.
A program may use at most 64 MiB of HBM per device.

```python
import jax
import jax.numpy as jnp
from jax import lax

LEAF = 512
RANK = 96
COLS = 64
LEVELS = 9
ORDER = 262144


def draw_row_basis(key, part):
    levels = jnp.arange(LEVELS).astype(jnp.float32)
    scales = (LEAF * 2.0 ** levels) ** (-0.5)
    base = jnp.clip(jax.random.normal(key, (LEVELS, RANK, ORDER), jnp.float32), -6.0, 6.0)
    return base * scales[:, None, None]


def level_of(key, extent, cuts, low, largest):
    level = 1.0
    for dim, shards_of in cuts:
        draws = jax.random.uniform(jax.random.fold_in(jax.random.fold_in(key, 6), dim), (shards_of,), jnp.float32, low / len(cuts), largest / len(cuts))
        level = level * jnp.repeat(jnp.exp(draws), extent[dim] // shards_of).reshape((-1,) + (1,) * (len(extent) - 1 - dim))
    return level


def bell_draw(stream_key, extent, spread, limit, shards=(), kind=jnp.bfloat16):
    values = jax.random.normal(stream_key, extent, jnp.float32) * spread
    if len(shards) > 0:
        values = level_of(stream_key, extent, shards, -0.22, 0.18) * values
    return jnp.clip(values, min=-limit, max=limit).astype(kind)


def setup_inputs(seed: int = 0) -> dict:
    key_list = jax.random.split(jax.random.key(seed), 7)
    return {
        "solution": bell_draw(key_list[0], (COLS, ORDER), 1.0, 6.0, ((1, 256),), jnp.float32),
        "incident": bell_draw(key_list[1], (COLS, ORDER), 2.0, 12.0, ((1, 256),), jnp.float32),
        "leaf_blocks": bell_draw(key_list[2], (LEAF, ORDER), LEAF ** -0.5, 0.25, ((1, 256),), jnp.float32),
        "leaf_inverse": bell_draw(key_list[3], (LEAF, ORDER), LEAF ** -0.5, 0.25, ((1, 256),), jnp.float32),
        "col_basis": bell_draw(key_list[4], (LEVELS, RANK, ORDER), RANK ** -0.5, 0.625, ((2, 256),), jnp.float32),
        "row_basis": draw_row_basis(jax.random.fold_in(key_list[6], 71), 0),
    }


def leaf_apply(field, blocks):
    cols, order = field.shape
    leaf = blocks.shape[0]
    count = order // leaf
    pieces = field.reshape(cols, count, leaf)
    tables = blocks.reshape(leaf, count, leaf)
    image = jnp.einsum("pkj,jki->pki", pieces, tables, precision=lax.Precision.HIGHEST)
    return image.reshape(cols, order)


def operator(field, leaf_blocks, col_basis, row_basis):
    cols, order = field.shape
    leaf = leaf_blocks.shape[0]
    image = leaf_apply(field, leaf_blocks)
    for level in range(LEVELS):
        node = leaf * 2 ** level
        count = order // node
        pieces = field.reshape(cols, count, node)
        rights = row_basis[level].reshape(RANK, count, node)
        coefs = jnp.einsum("pks,rks->kpr", pieces, rights, precision=lax.Precision.HIGHEST)
        coefs = coefs.reshape(count // 2, 2, cols, RANK)[:, ::-1].reshape(count, cols, RANK)
        lefts = col_basis[level].reshape(RANK, count, node)
        image = image + jnp.einsum("kpr,rks->pks", coefs, lefts, precision=lax.Precision.HIGHEST).reshape(cols, order)
    return image


def reference(solution, incident, leaf_blocks, leaf_inverse, col_basis, row_basis):
    first_residual = incident - operator(solution, leaf_blocks, col_basis, row_basis)
    refined = solution + leaf_apply(first_residual, leaf_inverse)
    residual = incident - operator(refined, leaf_blocks, col_basis, row_basis)
    return refined, residual
```

```python
import functools

import jax
import jax.numpy as jnp
from jax import lax
from jax.experimental import pallas as pl
from jax.experimental.pallas import tpu as pltpu
from jax.sharding import PartitionSpec as P

MESH = pl.DeviceIdType.MESH
F32 = jnp.float32
BF16 = jnp.bfloat16
RANK = 96
COLS = 64
ROWS = 1024
LEAF = 512
HALF = 384
NEAR = (1, 2, 3, 4)
FAR = (8, 5, 6, 7)
FAR_LANE = {level: RANK * i for i, level in enumerate(FAR)}


def flip(value, mask):
    for bit in range(4):
        if mask >> bit & 1:
            value = value + (1 - 2 * ((value // (1 << bit)) % 2)) * (1 << bit)
    return value


def level_of(mask):
    return 5 + mask.bit_length() - 1


def tiles_of(level):
    low = FAR_LANE[level]
    return low // 128, (low + RANK - 1) // 128 + 1


def split(value):
    high = value.astype(BF16)
    low = (value - high.astype(F32)).astype(BF16)
    return high, low


def split_rows(src, high_ref, low_ref, step=32):
    @pl.loop(0, src.shape[0] // step)
    def _(i):
        rows = pl.ds(pl.multiple_of(i * step, step), step)
        high, low = split(src[rows, :])
        high_ref[rows, :] = high
        low_ref[rows, :] = low


def stack_split(value):
    high, low = split(value)
    return jnp.concatenate([high, low], axis=0)


def mul(stacked, high, low):
    top = jnp.dot(stacked, high, preferred_element_type=F32)
    return top[:COLS] + top[COLS:] + jnp.dot(stacked[:COLS], low, preferred_element_type=F32)


def mul_t(stacked, high, low):
    dims = (((1,), (1,)), ((), ()))
    top = lax.dot_general(stacked, high, dims, preferred_element_type=F32)
    return top[:COLS] + top[COLS:] + lax.dot_general(stacked[:COLS], low, dims, preferred_element_type=F32)


def kernel(sol_hbm, inc_hbm, leaf_hbm, inv_hbm, col_hbm, row_hbm, ref_hbm, res_hbm, *scratch):
    (sol, inc, leaf, inv, colf, rowf, col0, row0,
     leaf_h, leaf_l, inv_h, inv_l, col_h, col_l, row_h, row_l, col0_h, col0_l, row0_h, row0_l,
     base, refined, out,
     near, far, swap, mine, ring_far, sum_far, cross, fin_far, all_far,
     ring_near, fin_near, fin_four, all_near, all_four,
     in_sem, out_sem, send_sem, recv_sem) = scratch

    wide = lax.axis_index("wide")
    z = lax.axis_index("grp")
    core = wide % 2
    plane = wide // 2
    other = wide + 1 - 2 * core

    loads = {}

    def load(name, src, dst):
        copy = pltpu.make_async_copy(src, dst, in_sem.at[len(loads)])
        copy.start()
        loads[name] = copy

    load("sol", sol_hbm, sol)
    for i, level in enumerate(FAR):
        load(("row", i + 4), row_hbm.at[level], rowf.at[pl.ds(HALF + RANK * i, RANK)])
    for i, level in enumerate(NEAR):
        load(("row", i), row_hbm.at[level], rowf.at[pl.ds(RANK * i, RANK)])
    load("leaf", leaf_hbm, leaf)
    load("row0", row_hbm.at[0], row0)
    load("col0", col_hbm.at[0], col0)
    load("inc", inc_hbm, inc)
    for i, level in enumerate(NEAR + FAR):
        load(("col", i), col_hbm.at[level], colf.at[pl.ds(RANK * i, RANK)])
    load("inv", inv_hbm, inv)

    plus1, minus1 = (z + 1) % 8, (z + 7) % 8
    plus2, minus2 = (z + 2) % 8, (z + 6) % 8
    peers = [(other, z)]
    peers += [(wide, flip(z, m)) for m in range(1, 8)]
    peers += [(flip(plane, m) * 2 + core, z) for m in range(1, 16)]
    peers += [(other, k) for k in (plus1, minus1, plus2, minus2)]
    barrier = pltpu.get_barrier_semaphore()
    for peer in peers:
        pl.semaphore_signal(barrier, inc=1, device_id=peer, device_id_type=MESH)

    copies = []

    def send(turn, src, dst, device):
        index = len(copies)
        copy = pltpu.make_async_remote_copy(
            src_ref=src, dst_ref=dst, send_sem=send_sem.at[index], recv_sem=recv_sem.at[index],
            device_id=device, device_id_type=MESH)
        copy.start()
        copies.append(copy)
        return copy

    lane = lax.broadcasted_iota(jnp.int32, (8, 128), 1)
    slot = z % 4

    def exchange(turn, make_far, make_near, hidden, settle):
        near_t, far_t, swap_t, mine_t = near.at[turn], far.at[turn], swap.at[turn], mine.at[turn]
        ring_far_t, sum_far_t, cross_t = ring_far.at[turn], sum_far.at[turn], cross.at[turn]
        fin_far_t, all_far_t = fin_far.at[turn], all_far.at[turn]
        ring_near_t, fin_near_t, fin_four_t = ring_near.at[turn], fin_near.at[turn], fin_four.at[turn]
        all_near_t, all_four_t = all_near.at[turn], all_four.at[turn]

        far_t[...] = make_far()
        if turn == 0:
            pl.semaphore_wait(barrier, len(peers))
        theirs = pl.ds(pl.multiple_of(32 * (1 - core), 32), 32)
        ours = pl.ds(pl.multiple_of(32 * core, 32), 32)
        core_copy = send(turn, far_t.at[theirs], swap_t, (other, z))
        near_t[...] = make_near()
        core_copy.wait_recv()
        mine_t[...] = far_t[ours, :] + swap_t[...]

        far_ring = []
        for m in range(1, 8):
            dest = flip(z, m)
            rows = pl.ds(pl.multiple_of(8 * (dest % 4), 8), 8)
            far_ring.append(send(turn, mine_t.at[rows], ring_far_t.at[m], (wide, dest)))
        near_ring = []
        for m in range(1, 8):
            dest = flip(z, m)
            rows = pl.ds(pl.multiple_of(16 * (dest % 4), 16), 16)
            near_ring.append(send(turn, near_t.at[rows], ring_near_t.at[z], (wide, dest)))
        own16 = pl.ds(pl.multiple_of(16 * slot, 16), 16)
        own8 = pl.ds(pl.multiple_of(8 * slot, 8), 8)
        ring_near_t[z] = near_t[own16, :]

        hidden(0)

        for copy in far_ring:
            copy.wait_recv()
        total = mine_t[own8, :]
        for m in range(1, 8):
            total = total + ring_far_t[m]
        sum_far_t[...] = total

        plane_copies = []
        for m in sorted(range(1, 16), key=lambda m: -m):
            first, last = tiles_of(level_of(m))
            lanes = pl.ds(128 * first, 128 * (last - first))
            plane_copies.append(send(turn, sum_far_t.at[:, lanes], cross_t.at[m, :, lanes],
                                     (flip(plane, m) * 2 + core, z)))

        hidden(1)

        for copy in near_ring:
            copy.wait_recv()
        pair = [ring_near_t[2 * k] + ring_near_t[2 * k + 1] for k in range(4)]
        quad = [pair[0] + pair[1], pair[2] + pair[3]]
        lane16 = lax.broadcasted_iota(jnp.int32, (16, HALF), 1)
        readers = (z, plus1, minus1, plus2)
        for k, reader in enumerate(readers):
            one = ring_near_t[flip(reader, 1)]
            which = reader // 2
            two = jnp.where(which == 0, pair[1], jnp.where(which == 1, pair[0], jnp.where(which == 2, pair[3], pair[2])))
            three = jnp.where(reader // 4 == 0, quad[1], quad[0])
            fin_near_t[k] = jnp.where(lane16 < RANK, one, jnp.where(lane16 < 2 * RANK, two, three))
        fin_four_t[...] = (quad[0] + quad[1])[:, 256:]
        all_near_t[own16, :] = fin_near_t[0]
        near_same = [send(turn, fin_near_t.at[k], all_near_t.at[own16], (wide, readers[k])) for k in (1, 2, 3)]
        near_other = [send(turn, fin_four_t, all_four_t.at[own16], (other, readers[k])) for k in (0, 1, 2, 3)]

        for copy in plane_copies:
            copy.wait_recv()
        for tile in range(3):
            lanes = pl.ds(128 * tile, 128)
            value = jnp.zeros((8, 128), F32)
            for level in FAR:
                first, last = tiles_of(level)
                if not first <= tile < last:
                    continue
                part = None
                for m in range(1, 16):
                    if level_of(m) == level:
                        piece = cross_t[m, :, lanes]
                        part = piece if part is None else part + piece
                low = FAR_LANE[level] - 128 * tile
                inside = jnp.logical_and(lane >= low, lane < low + RANK)
                value = jnp.where(inside, part, value)
            fin_far_t[:, lanes] = value
        own_far = pl.ds(pl.multiple_of(32 * core + 8 * slot, 8), 8)
        all_far_t[own_far, :] = fin_far_t[...]
        far_gather = []
        for k in (3, 1, 2):
            far_gather.append(send(turn, fin_far_t, all_far_t.at[own_far], (wide, readers[k])))
            far_gather.append(send(turn, fin_far_t, all_far_t.at[own_far], (other, readers[k])))
        far_gather.append(send(turn, fin_far_t, all_far_t.at[own_far], (other, z)))

        for copy in near_same + near_other:
            copy.wait_recv()
        lane64 = lax.broadcasted_iota(jnp.int32, (COLS, 128), 1)
        last = jnp.where(lane64 < 32, all_near_t[:, 256:], all_four_t[...])
        coefs_near = jnp.concatenate([all_near_t[:, :256], last], axis=1)
        settle(0, coefs_near)
        for copy in far_gather:
            copy.wait_recv()
        settle(1, all_far_t[...])

    def far_part(stacked):
        return mul_t(stacked, row_h[HALF:, :], row_l[HALF:, :])

    def near_part(stacked):
        return mul_t(stacked, row_h[:HALF, :], row_l[:HALF, :])

    def local_image(stacked):
        coefs = []
        for h in range(2):
            cols = slice(LEAF * h, LEAF * (h + 1))
            coefs.append(stack_split(mul_t(stacked[:, cols], row0_h[:, cols], row0_l[:, cols])))
        parts = []
        for h in range(2):
            cols = slice(LEAF * h, LEAF * (h + 1))
            image = mul(stacked[:, cols], leaf_h[:, cols], leaf_l[:, cols])
            parts.append(image + mul(coefs[1 - h], col0_h[:, cols], col0_l[:, cols]))
        return jnp.concatenate(parts, axis=1)

    def far_image(group, coefs):
        rows = slice(HALF * group, HALF * (group + 1))
        return mul(stack_split(coefs), col_h[rows, :], col_l[rows, :])

    loads["sol"].wait()
    sol_s = stack_split(sol[...])

    def first_far():
        for i in range(4, 8):
            loads[("row", i)].wait()
        split_rows(rowf.at[pl.ds(HALF, HALF)], row_h.at[pl.ds(HALF, HALF)], row_l.at[pl.ds(HALF, HALF)])
        return far_part(sol_s)

    def first_near():
        for i in range(4):
            loads[("row", i)].wait()
        split_rows(rowf.at[pl.ds(0, HALF)], row_h.at[pl.ds(0, HALF)], row_l.at[pl.ds(0, HALF)])
        return near_part(sol_s)

    def first_hidden(stage):
        if stage == 0:
            for name in ("leaf", "row0", "col0", "inc"):
                loads[name].wait()
            split_rows(leaf, leaf_h, leaf_l)
            split_rows(row0, row0_h, row0_l)
            split_rows(col0, col0_h, col0_l)
            base[...] = inc[...] - local_image(sol_s)
        else:
            for i in range(8):
                loads[("col", i)].wait()
            split_rows(colf, col_h, col_l)
            loads["inv"].wait()
            split_rows(inv, inv_h, inv_l)

    def first_settle(group, coefs):
        base[...] = base[...] - far_image(group, coefs)

    exchange(0, first_far, first_near, first_hidden, first_settle)

    residual_s = stack_split(base[...])
    for h in range(2):
        cols = slice(LEAF * h, LEAF * (h + 1))
        refined[:, cols] = sol[:, cols] + mul(residual_s[:, cols], inv_h[:, cols], inv_l[:, cols])
    ref_copy = pltpu.make_async_copy(refined, ref_hbm, out_sem.at[0])
    ref_copy.start()
    refined_s = stack_split(refined[...])

    def second_hidden(stage):
        if stage == 0:
            out[...] = inc[...] - local_image(refined_s)

    def second_settle(group, coefs):
        out[...] = out[...] - far_image(group, coefs)

    exchange(1, lambda: far_part(refined_s), lambda: near_part(refined_s), second_hidden, second_settle)

    res_copy = pltpu.make_async_copy(out, res_hbm, out_sem.at[1])
    res_copy.start()
    for copy in copies:
        copy.wait_send()
    ref_copy.wait()
    res_copy.wait()


def per_device(solution, incident, leaf_blocks, leaf_inverse, col_basis, row_basis):
    vmem = pltpu.VMEM
    n_copies = 2 * (1 + 7 + 7 + 15 + 3 + 4 + 7)
    scratch = [
        vmem((COLS, ROWS), F32), vmem((COLS, ROWS), F32), vmem((LEAF, ROWS), F32), vmem((LEAF, ROWS), F32),
        vmem((2 * HALF, ROWS), F32), vmem((2 * HALF, ROWS), F32), vmem((RANK, ROWS), F32), vmem((RANK, ROWS), F32),
        vmem((LEAF, ROWS), BF16), vmem((LEAF, ROWS), BF16), vmem((LEAF, ROWS), BF16), vmem((LEAF, ROWS), BF16),
        vmem((2 * HALF, ROWS), BF16), vmem((2 * HALF, ROWS), BF16),
        vmem((2 * HALF, ROWS), BF16), vmem((2 * HALF, ROWS), BF16),
        vmem((RANK, ROWS), BF16), vmem((RANK, ROWS), BF16), vmem((RANK, ROWS), BF16), vmem((RANK, ROWS), BF16),
        vmem((COLS, ROWS), F32), vmem((COLS, ROWS), F32), vmem((COLS, ROWS), F32),
        vmem((2, COLS, HALF), F32),
        vmem((2, COLS, HALF), F32),
        vmem((2, 32, HALF), F32),
        vmem((2, 32, HALF), F32),
        vmem((2, 8, 8, HALF), F32),
        vmem((2, 8, HALF), F32),
        vmem((2, 16, 8, HALF), F32),
        vmem((2, 8, HALF), F32),
        vmem((2, COLS, HALF), F32),
        vmem((2, 8, 16, HALF), F32),
        vmem((2, 4, 16, HALF), F32),
        vmem((2, 16, 128), F32),
        vmem((2, COLS, HALF), F32),
        vmem((2, COLS, 128), F32),
        pltpu.SemaphoreType.DMA((24,)),
        pltpu.SemaphoreType.DMA((2,)),
        pltpu.SemaphoreType.DMA((n_copies,)),
        pltpu.SemaphoreType.DMA((n_copies,)),
    ]
    anywhere = pl.BlockSpec(memory_space=pl.ANY)
    shape = jax.ShapeDtypeStruct((COLS, ROWS), F32)
    return pl.pallas_call(
        kernel,
        out_shape=(shape, shape),
        in_specs=[anywhere] * 6,
        out_specs=(anywhere, anywhere),
        scratch_shapes=scratch,
        compiler_params=pltpu.CompilerParams(
            collective_id=0, has_side_effects=True, vmem_limit_bytes=60 * 1024 * 1024),
    )(solution, incident, leaf_blocks, leaf_inverse, col_basis, row_basis)


def solution(mesh):
    in_specs = (
        P(None, ("wide", "grp")),
        P(None, ("wide", "grp")),
        P(None, ("wide", "grp")),
        P(None, ("wide", "grp")),
        P(None, None, ("wide", "grp")),
        P(None, None, ("wide", "grp")),
    )
    out_specs = (P(None, ("wide", "grp")), P(None, ("wide", "grp")))
    return jax.shard_map(
        per_device, mesh=mesh, in_specs=in_specs, out_specs=out_specs, check_vma=False
    )
```

```python
import functools

import jax
import jax.numpy as jnp
from jax import lax
from jax.experimental import pallas as pl
from jax.experimental.pallas import tpu as pltpu
from jax.sharding import PartitionSpec as P

MESH = pl.DeviceIdType.MESH
F32 = jnp.float32
BF16 = jnp.bfloat16
RANK = 96
COLS = 64
ROWS = 1024
LEAF = 512
HALF = 384
NEAR = (1, 2, 3, 4)
FAR = (8, 5, 6, 7)
FAR_LANE = {level: RANK * i for i, level in enumerate(FAR)}


def flip(value, mask):
    for bit in range(4):
        if mask >> bit & 1:
            value = value + (1 - 2 * ((value // (1 << bit)) % 2)) * (1 << bit)
    return value


RING = (4, 3, 5, 2, 6, 1, 7)
HOPS = (0, 1, 2, 1)
PLANE = tuple(sorted(range(1, 16), key=lambda m: -(HOPS[m % 4] + HOPS[m // 4])))
NEAR_PEERS = (4, 5, 6, 7, 2, 3, 1)


def near_level(mask):
    return mask.bit_length()


def level_of(mask):
    return 5 + mask.bit_length() - 1


def tiles_of(level):
    low = FAR_LANE[level]
    return low // 128, (low + RANK - 1) // 128 + 1


def split(value):
    high = value.astype(BF16)
    low = (value - high.astype(F32)).astype(BF16)
    return high, low


def split_rows(src, high_ref, low_ref, step=32):
    @pl.loop(0, src.shape[0] // step)
    def _(i):
        rows = pl.ds(pl.multiple_of(i * step, step), step)
        high, low = split(src[rows, :])
        high_ref[rows, :] = high
        low_ref[rows, :] = low


def stack_split(value):
    high, low = split(value)
    return jnp.concatenate([high, low], axis=0)


def mul(stacked, high, low):
    top = jnp.dot(stacked, high, preferred_element_type=F32)
    return top[:COLS] + top[COLS:] + jnp.dot(stacked[:COLS], low, preferred_element_type=F32)


def mul_t(stacked, high, low):
    dims = (((1,), (1,)), ((), ()))
    top = lax.dot_general(stacked, high, dims, preferred_element_type=F32)
    return top[:COLS] + top[COLS:] + lax.dot_general(stacked[:COLS], low, dims, preferred_element_type=F32)


def pack(value):
    lane = lax.broadcasted_iota(jnp.int32, (16, 128), 1)
    rest = value[48:]
    rows = [jnp.where(lane < RANK, value[16 * j:16 * j + 16], pltpu.roll(rest, RANK - 32 * j, 1)) for j in range(3)]
    return jnp.concatenate(rows, axis=0)


def unpack(value):
    lane = lax.broadcasted_iota(jnp.int32, (16, 128), 1)
    moved = [pltpu.roll(value[16 * j:16 * j + 16], 32 * j + 32, 1) for j in range(3)]
    rest = jnp.where(lane < 32, moved[0], jnp.where(lane < 64, moved[1], moved[2]))
    return jnp.concatenate([value, rest], axis=0)


def apart(dense):
    lane = lax.broadcasted_iota(jnp.int32, (COLS, 128), 1)
    t0, t1, t2 = dense[:, :128], dense[:, 128:256], dense[:, 256:]
    return (t0, pltpu.roll(jnp.where(lane >= 96, t0, t1), 32, 1),
            pltpu.roll(jnp.where(lane >= 64, t1, t2), 64, 1), pltpu.roll(t2, 96, 1))


def together(c1, c2, c3, c4):
    lane = lax.broadcasted_iota(jnp.int32, (COLS, 128), 1)
    c2, c3, c4 = pltpu.roll(c2, 96, 1), pltpu.roll(c3, 64, 1), pltpu.roll(c4, 32, 1)
    return jnp.concatenate(
        [jnp.where(lane < 96, c1, c2), jnp.where(lane < 64, c2, c3), jnp.where(lane < 32, c3, c4)], axis=1)


def kernel(sol_hbm, inc_hbm, leaf_hbm, inv_hbm, col_hbm, row_hbm, refined, out, *scratch):
    (sol, inc, leaf, inv, colf, rowf, col0, row0,
     leaf_h, leaf_l, inv_h, inv_l, col_h, col_l, row_h, row_l, col0_h, col0_l, row0_h, row0_l,
     mid_h, mid_l, map_h, map_l, base, ahead,
     near, four, far, swap, mine, ring_far, sum_far, cross, fin_far, all_far,
     near_in, ring_four, fin_four, all_four,
     in_sem, send_sem, recv_sem) = scratch

    wide = lax.axis_index("wide")
    z = lax.axis_index("grp")
    core = wide % 2
    plane = wide // 2
    other = wide + 1 - 2 * core

    plus1, minus1 = (z + 1) % 8, (z + 7) % 8
    plus2, minus2 = (z + 2) % 8, (z + 6) % 8
    peers = [(flip(plane, m) * 2 + core, z) for m in PLANE]
    peers += [(wide, (z + k) % 8) for k in RING]
    peers += [(other, k) for k in (plus2, minus2, plus1, minus1)]
    peers += [(other, z)]
    barrier = pltpu.get_barrier_semaphore()
    for peer in peers:
        pl.semaphore_signal(barrier, inc=1, device_id=peer, device_id_type=MESH)

    loads = {}

    def load(name, src, dst):
        copy = pltpu.make_async_copy(src, dst, in_sem.at[len(loads)])
        copy.start()
        loads[name] = copy

    load("sol", sol_hbm, sol)
    for i, level in enumerate(FAR):
        load(("row", i + 4), row_hbm.at[level], rowf.at[pl.ds(HALF + RANK * i, RANK)])
    for i, level in enumerate(NEAR):
        load(("row", i), row_hbm.at[level], rowf.at[pl.ds(RANK * i, RANK)])
    load("leaf", leaf_hbm, leaf)
    load("row0", row_hbm.at[0], row0)
    load("col0", col_hbm.at[0], col0)
    load("inc", inc_hbm, inc)
    load("inv", inv_hbm, inv)
    for i, level in enumerate(NEAR + FAR):
        load(("col", i), col_hbm.at[level], colf.at[pl.ds(RANK * i, RANK)])

    copies = []

    def send(src, dst, device):
        index = len(copies)
        copy = pltpu.make_async_remote_copy(
            src_ref=src, dst_ref=dst, send_sem=send_sem.at[index], recv_sem=recv_sem.at[index],
            device_id=device, device_id_type=MESH)
        copy.start()
        copies.append(copy)
        return copy

    lane = lax.broadcasted_iota(jnp.int32, (8, 128), 1)
    slot = z % 4
    beyond = (z + 2 + 4 * core) % 8
    readers = (beyond, plus1, minus1)

    def exchange(turn, make_far, during_core, make_near, hidden, settle):
        near_t, four_t, far_t, swap_t, mine_t = near.at[turn], four.at[turn], far.at[turn], swap.at[turn], mine.at[turn]
        ring_far_t, sum_far_t, cross_t = ring_far.at[turn], sum_far.at[turn], cross.at[turn]
        fin_far_t, all_far_t = fin_far.at[turn], all_far.at[turn]
        near_in_t, ring_four_t, fin_four_t, all_four_t = near_in.at[turn], ring_four.at[turn], fin_four.at[turn], all_four.at[turn]

        far_t[...] = make_far()
        if turn == 0:
            pl.semaphore_wait(barrier, len(peers))
        theirs = pl.ds(pl.multiple_of(32 * (1 - core), 32), 32)
        ours = pl.ds(pl.multiple_of(32 * core, 32), 32)
        core_copy = send(far_t.at[theirs], swap_t, (other, z))
        during_core()
        core_copy.wait_recv()
        mine_t[...] = far_t[ours, :] + swap_t[...]

        far_ring = []
        for k in RING:
            dest = (z + k) % 8
            rows = pl.ds(pl.multiple_of(8 * (dest % 4), 8), 8)
            far_ring.append(send(mine_t.at[rows], ring_far_t.at[k], (wide, dest)))

        levels = apart(make_near())
        four_t[...] = levels[3]
        for level in (1, 2, 3):
            near_t[level] = pack(levels[level - 1])
        four_ring = []
        for k in RING:
            dest = (z + k) % 8
            rows = pl.ds(pl.multiple_of(16 * (dest % 4), 16), 16)
            four_ring.append(send(four_t.at[rows], ring_four_t.at[k], (wide, dest)))
        near_copies = []
        for m in NEAR_PEERS:
            near_copies.append(send(near_t.at[near_level(m)], near_in_t.at[m], (wide, flip(z, m))))

        hidden(0)

        own16 = pl.ds(pl.multiple_of(16 * slot, 16), 16)
        own8 = pl.ds(pl.multiple_of(8 * slot, 8), 8)
        for copy in far_ring:
            copy.wait_recv()
        total = mine_t[own8, :]
        for k in range(1, 8):
            total = total + ring_far_t[k]
        sum_far_t[...] = total

        plane_copies = []
        for m in PLANE:
            first, last = tiles_of(level_of(m))
            lanes = pl.ds(128 * first, 128 * (last - first))
            plane_copies.append(send(sum_far_t.at[:, lanes], cross_t.at[m, :, lanes],
                                     (flip(plane, m) * 2 + core, z)))

        for copy in four_ring:
            copy.wait_recv()
        total = four_t[own16, :]
        for k in range(1, 8):
            total = total + ring_four_t[k]
        fin_four_t[...] = total
        four_gather = [send(fin_four_t, all_four_t.at[own16], (other, reader)) for reader in readers]
        four_gather.append(send(fin_four_t, all_four_t.at[own16], (other, z)))

        hidden(1)

        for copy in plane_copies:
            copy.wait_recv()
        for tile in range(3):
            lanes = pl.ds(128 * tile, 128)
            value = jnp.zeros((8, 128), F32)
            for level in FAR:
                first, last = tiles_of(level)
                if not first <= tile < last:
                    continue
                part = None
                for m in range(1, 16):
                    if level_of(m) == level:
                        piece = cross_t[m, :, lanes]
                        part = piece if part is None else part + piece
                low = FAR_LANE[level] - 128 * tile
                inside = jnp.logical_and(lane >= low, lane < low + RANK)
                value = jnp.where(inside, part, value)
            fin_far_t[:, lanes] = value
        own_far = pl.ds(pl.multiple_of(32 * core + 8 * slot, 8), 8)
        far_gather = []
        for reader in readers:
            far_gather.append(send(fin_far_t, all_far_t.at[own_far], (wide, reader)))
            far_gather.append(send(fin_far_t, all_far_t.at[own_far], (other, reader)))
        far_gather.append(send(fin_far_t, all_far_t.at[own_far], (other, z)))
        all_far_t[own_far, :] = fin_far_t[...]

        for copy in near_copies + four_gather:
            copy.wait_recv()
        c1 = unpack(near_in_t[1])
        c2 = unpack(near_in_t[2] + near_in_t[3])
        c3 = unpack((near_in_t[4] + near_in_t[5]) + (near_in_t[6] + near_in_t[7]))
        settle(0, together(c1, c2, c3, all_four_t[...]))
        for copy in far_gather:
            copy.wait_recv()
        settle(1, all_far_t[...])

    def far_part(stacked):
        return mul_t(stacked, row_h[HALF:, :], row_l[HALF:, :])

    def near_part(stacked):
        return mul_t(stacked, row_h[:HALF, :], row_l[:HALF, :])

    def local_image(stacked):
        coefs = []
        for h in range(2):
            cols = slice(LEAF * h, LEAF * (h + 1))
            coefs.append(stack_split(mul_t(stacked[:, cols], row0_h[:, cols], row0_l[:, cols])))
        parts = []
        for h in range(2):
            cols = slice(LEAF * h, LEAF * (h + 1))
            image = mul(stacked[:, cols], leaf_h[:, cols], leaf_l[:, cols])
            parts.append(image + mul(coefs[1 - h], col0_h[:, cols], col0_l[:, cols]))
        return jnp.concatenate(parts, axis=1)

    def far_image(group, coefs):
        rows = slice(HALF * group, HALF * (group + 1))
        return mul(stack_split(coefs), col_h[rows, :], col_l[rows, :])

    def refine():
        residual_s = stack_split(base[...])
        parts = []
        for h in range(2):
            cols = slice(LEAF * h, LEAF * (h + 1))
            parts.append(sol[:, cols] + mul(residual_s[:, cols], inv_h[:, cols], inv_l[:, cols]))
        return jnp.concatenate(parts, axis=1)

    loads["sol"].wait()
    sol_s = stack_split(sol[...])

    def first_far():
        for i in range(4, 8):
            loads[("row", i)].wait()
        split_rows(rowf.at[pl.ds(HALF, HALF)], row_h.at[pl.ds(HALF, HALF)], row_l.at[pl.ds(HALF, HALF)])
        return far_part(sol_s)

    near_value = []

    def first_during():
        for i in range(4):
            loads[("row", i)].wait()
        split_rows(rowf.at[pl.ds(0, HALF)], row_h.at[pl.ds(0, HALF)], row_l.at[pl.ds(0, HALF)])
        near_value.append(near_part(sol_s))

    def first_hidden(stage):
        if stage == 0:
            for name in ("leaf", "row0", "col0", "inc"):
                loads[name].wait()
            split_rows(leaf, leaf_h, leaf_l)
            split_rows(row0, row0_h, row0_l)
            split_rows(col0, col0_h, col0_l)
            base[...] = inc[...] - local_image(sol_s)
            loads["inv"].wait()
            split_rows(inv, inv_h, inv_l)
            for i in range(8):
                loads[("col", i)].wait()
            split_rows(colf, col_h, col_l)
            for h in range(2):
                for n in range(2):
                    rows = slice(LEAF * h, LEAF * (h + 1))
                    cols = slice(LEAF * h + 256 * n, LEAF * h + 256 * (n + 1))
                    value = jnp.dot(col_h[HALF:, rows], inv_h[:, cols], preferred_element_type=F32)
                    value = value + jnp.dot(col_l[HALF:, rows], inv_h[:, cols], preferred_element_type=F32)
                    value = value + jnp.dot(col_h[HALF:, rows], inv_l[:, cols], preferred_element_type=F32)
                    high, low = split(value)
                    mid_h[:, cols] = high
                    mid_l[:, cols] = low
        else:
            dims = (((1,), (1,)), ((), ()))
            for n in range(3):
                cols = slice(128 * n, 128 * (n + 1))
                rows = slice(HALF + 128 * n, HALF + 128 * (n + 1))
                value = lax.dot_general(mid_h[...], row_h[rows, :], dims, preferred_element_type=F32)
                value = value + lax.dot_general(mid_l[...], row_h[rows, :], dims, preferred_element_type=F32)
                value = value + lax.dot_general(mid_h[...], row_l[rows, :], dims, preferred_element_type=F32)
                high, low = split(value)
                map_h[:, cols] = high
                map_l[:, cols] = low

    coefs_far = []

    def first_settle(group, coefs):
        if group == 0:
            base[...] = base[...] - far_image(0, coefs)
            ahead[...] = far_part(stack_split(refine()))
        else:
            coefs_far.append(stack_split(coefs))

    exchange(0, first_far, first_during, lambda: near_value[0], first_hidden, first_settle)

    def second_far():
        return ahead[...] - mul(coefs_far[0], map_h[...], map_l[...])

    def second_during():
        base[...] = base[...] - mul(coefs_far[0], col_h[HALF:, :], col_l[HALF:, :])
        refined[...] = refine()

    def second_near():
        return near_part(stack_split(refined[...]))

    def second_hidden(stage):
        if stage == 0:
            out[...] = inc[...] - local_image(stack_split(refined[...]))

    def second_settle(group, coefs):
        out[...] = out[...] - far_image(group, coefs)

    exchange(1, second_far, second_during, second_near, second_hidden, second_settle)

    for copy in copies:
        copy.wait_send()


def per_device(solution, incident, leaf_blocks, leaf_inverse, col_basis, row_basis):
    vmem = pltpu.VMEM
    n_copies = 2 * (1 + 7 + 7 + 7 + 15 + 4 + 7)
    scratch = [
        vmem((COLS, ROWS), F32), vmem((COLS, ROWS), F32), vmem((LEAF, ROWS), F32), vmem((LEAF, ROWS), F32),
        vmem((2 * HALF, ROWS), F32), vmem((2 * HALF, ROWS), F32), vmem((RANK, ROWS), F32), vmem((RANK, ROWS), F32),
        vmem((LEAF, ROWS), BF16), vmem((LEAF, ROWS), BF16), vmem((LEAF, ROWS), BF16), vmem((LEAF, ROWS), BF16),
        vmem((2 * HALF, ROWS), BF16), vmem((2 * HALF, ROWS), BF16),
        vmem((2 * HALF, ROWS), BF16), vmem((2 * HALF, ROWS), BF16),
        vmem((RANK, ROWS), BF16), vmem((RANK, ROWS), BF16), vmem((RANK, ROWS), BF16), vmem((RANK, ROWS), BF16),
        vmem((HALF, ROWS), BF16), vmem((HALF, ROWS), BF16),
        vmem((HALF, HALF), BF16), vmem((HALF, HALF), BF16),
        vmem((COLS, ROWS), F32),
        vmem((COLS, HALF), F32),
        vmem((2, 4, 48, 128), F32),
        vmem((2, COLS, 128), F32),
        vmem((2, COLS, HALF), F32),
        vmem((2, 32, HALF), F32),
        vmem((2, 32, HALF), F32),
        vmem((2, 8, 8, HALF), F32),
        vmem((2, 8, HALF), F32),
        vmem((2, 16, 8, HALF), F32),
        vmem((2, 8, HALF), F32),
        vmem((2, COLS, HALF), F32),
        vmem((2, 8, 48, 128), F32),
        vmem((2, 8, 16, 128), F32),
        vmem((2, 16, 128), F32),
        vmem((2, COLS, 128), F32),
        pltpu.SemaphoreType.DMA((24,)),
        pltpu.SemaphoreType.DMA((n_copies,)),
        pltpu.SemaphoreType.DMA((n_copies,)),
    ]
    anywhere = pl.BlockSpec(memory_space=pltpu.HBM)
    resident = pl.BlockSpec(memory_space=pltpu.VMEM)
    shape = jax.ShapeDtypeStruct((COLS, ROWS), F32)
    return pl.pallas_call(
        kernel,
        out_shape=(shape, shape),
        in_specs=[anywhere] * 6,
        out_specs=(resident, resident),
        scratch_shapes=scratch,
        compiler_params=pltpu.CompilerParams(
            collective_id=0, has_side_effects=True, vmem_limit_bytes=36 * 1024 * 1024),
    )(*(pltpu.with_memory_space_constraint(x, pltpu.HBM) for x in (
        solution, incident, leaf_blocks, leaf_inverse, col_basis, row_basis)))


def solution(mesh):
    in_specs = (
        P(None, ("wide", "grp")),
        P(None, ("wide", "grp")),
        P(None, ("wide", "grp")),
        P(None, ("wide", "grp")),
        P(None, None, ("wide", "grp")),
        P(None, None, ("wide", "grp")),
    )
    out_specs = (P(None, ("wide", "grp")), P(None, ("wide", "grp")))
    return jax.shard_map(
        per_device, mesh=mesh, in_specs=in_specs, out_specs=out_specs, check_vma=False
    )
```

```python
import functools

import jax
import jax.numpy as jnp
from jax import lax
from jax.experimental import pallas as pl
from jax.experimental.pallas import tpu as pltpu
from jax.sharding import PartitionSpec as P

MESH = pl.DeviceIdType.MESH
F32 = jnp.float32
BF16 = jnp.bfloat16
RANK = 96
COLS = 64
ROWS = 1024
LEAF = 512
HALF = 384
NEAR = (1, 2, 3, 4)
FAR = (8, 5, 6, 7)
FAR_LANE = {level: RANK * i for i, level in enumerate(FAR)}


def flip(value, mask):
    for bit in range(4):
        if mask >> bit & 1:
            value = value + (1 - 2 * ((value // (1 << bit)) % 2)) * (1 << bit)
    return value


RING = (4, 3, 5, 2, 6, 1, 7)
HOPS = (0, 1, 2, 1)
PLANE = tuple(sorted(range(1, 16), key=lambda m: -(HOPS[m % 4] + HOPS[m // 4])))
NEAR_PEERS = (4, 5, 6, 7, 2, 3, 1)


def near_level(mask):
    return mask.bit_length()


def level_of(mask):
    return 5 + mask.bit_length() - 1


def tiles_of(level):
    low = FAR_LANE[level]
    return low // 128, (low + RANK - 1) // 128 + 1


CROSS = tuple((m, tile) for m in PLANE for tile in range(*tiles_of(level_of(m))))


def split(value):
    high = value.astype(BF16)
    low = (value - high.astype(F32)).astype(BF16)
    return high, low


def split_rows(src, high_ref, low_ref, step=32, cols=slice(None)):
    @pl.loop(0, src.shape[0] // step)
    def _(i):
        rows = pl.ds(pl.multiple_of(i * step, step), step)
        high, low = split(src[rows, cols])
        high_ref[rows, cols] = high
        low_ref[rows, cols] = low


def stack_split(value):
    high, low = split(value)
    return jnp.concatenate([high, low], axis=0)


def mul(stacked, high, low):
    top = jnp.dot(stacked, high, preferred_element_type=F32)
    return top[:COLS] + top[COLS:] + jnp.dot(stacked[:COLS], low, preferred_element_type=F32)


def mul_t(stacked, high, low):
    dims = (((1,), (1,)), ((), ()))
    top = lax.dot_general(stacked, high, dims, preferred_element_type=F32)
    return top[:COLS] + top[COLS:] + lax.dot_general(stacked[:COLS], low, dims, preferred_element_type=F32)


def pack(value):
    lane = lax.broadcasted_iota(jnp.int32, (16, 128), 1)
    rest = value[48:]
    rows = [jnp.where(lane < RANK, value[16 * j:16 * j + 16], pltpu.roll(rest, RANK - 32 * j, 1)) for j in range(3)]
    return jnp.concatenate(rows, axis=0)


def unpack(value):
    lane = lax.broadcasted_iota(jnp.int32, (16, 128), 1)
    moved = [pltpu.roll(value[16 * j:16 * j + 16], 32 * j + 32, 1) for j in range(3)]
    rest = jnp.where(lane < 32, moved[0], jnp.where(lane < 64, moved[1], moved[2]))
    return jnp.concatenate([value, rest], axis=0)


def apart(dense):
    lane = lax.broadcasted_iota(jnp.int32, (COLS, 128), 1)
    t0, t1, t2 = dense[:, :128], dense[:, 128:256], dense[:, 256:]
    return (t0, pltpu.roll(jnp.where(lane >= 96, t0, t1), 32, 1),
            pltpu.roll(jnp.where(lane >= 64, t1, t2), 64, 1), pltpu.roll(t2, 96, 1))


def together(c1, c2, c3, c4):
    lane = lax.broadcasted_iota(jnp.int32, (COLS, 128), 1)
    c2, c3, c4 = pltpu.roll(c2, 96, 1), pltpu.roll(c3, 64, 1), pltpu.roll(c4, 32, 1)
    return jnp.concatenate(
        [jnp.where(lane < 96, c1, c2), jnp.where(lane < 64, c2, c3), jnp.where(lane < 32, c3, c4)], axis=1)


def kernel(sol_hbm, inc_hbm, leaf_hbm, inv_hbm, col_hbm, row_hbm, refined, out, *scratch):
    (sol, inc, leaf, inv, colf, rowf, col0, row0,
     leaf_h, leaf_l, inv_h, inv_l, col_h, col_l, row_h, row_l, col0_h, col0_l, row0_h, row0_l,
     mid_h, mid_l, map_h, map_l, base, ahead,
     near, four, far, swap, mine, ring_far, sum_far, cross, fin_far, all_far,
     near_in, ring_four, fin_four, all_four,
     in_sem, send_sem, recv_sem) = scratch

    wide = lax.axis_index("wide")
    z = lax.axis_index("grp")
    core = wide % 2
    plane = wide // 2
    other = wide + 1 - 2 * core

    names = []

    def load(name, pairs, whole):
        sem = in_sem.at[len(names)]
        names.append(name)
        for src, dst in pairs:
            pltpu.make_async_copy(src, dst, sem).start()
        loads[name] = pltpu.make_async_copy(whole, whole, sem)

    loads = {}
    load("sol", [(sol_hbm, sol)], sol)
    for h in range(2):
        cols = pl.ds(LEAF * h, LEAF)
        load(("far", h), [(row_hbm.at[level, :, cols], rowf.at[pl.ds(HALF + RANK * i, RANK), cols])
                          for i, level in enumerate(FAR)], rowf.at[pl.ds(HALF, HALF), cols])

    plus1, minus1 = (z + 1) % 8, (z + 7) % 8
    plus2, minus2 = (z + 2) % 8, (z + 6) % 8
    peers = [(flip(plane, m) * 2 + core, z) for m in PLANE]
    peers += [(wide, (z + k) % 8) for k in RING]
    peers += [(other, k) for k in (plus2, minus2, plus1, minus1)]
    peers += [(other, z)]
    peers = peers[:1] + peers[15:18] + peers[1:15] + peers[18:]
    barrier = pltpu.get_barrier_semaphore()
    for peer in peers:
        pl.semaphore_signal(barrier, inc=1, device_id=peer, device_id_type=MESH)

    load("near", [(row_hbm.at[level], rowf.at[pl.ds(RANK * i, RANK)]) for i, level in enumerate(NEAR)],
         rowf.at[pl.ds(0, HALF)])
    load("leaf", [(leaf_hbm, leaf)], leaf)
    load("row0", [(row_hbm.at[0], row0)], row0)
    load("col0", [(col_hbm.at[0], col0)], col0)
    load("inc", [(inc_hbm, inc)], inc)
    load("inv", [(inv_hbm, inv)], inv)
    load("col", [(col_hbm.at[level], colf.at[pl.ds(RANK * i, RANK)]) for i, level in enumerate(NEAR + FAR)], colf)

    groups = []

    class Group:
        def __init__(self, whole):
            self.send_sem = send_sem.at[len(groups)]
            self.recv_sem = recv_sem.at[len(groups)]
            self.whole = whole
            groups.append(self)

        def send(self, src, dst, device):
            pltpu.make_async_remote_copy(
                src_ref=src, dst_ref=dst, send_sem=self.send_sem, recv_sem=self.recv_sem,
                device_id=device, device_id_type=MESH).start()

        def wait_recv(self):
            pltpu.make_async_copy(self.whole, self.whole, self.recv_sem).wait()

        def wait_send(self):
            pltpu.make_async_copy(self.whole, self.whole, self.send_sem).wait()

    lane = lax.broadcasted_iota(jnp.int32, (8, 128), 1)
    slot = z % 4
    beyond = (z + 2 + 4 * core) % 8
    readers = (beyond, plus1, minus1)

    def exchange(turn, make_far, during_core, make_near, hidden, settle):
        near_t, four_t, far_t, swap_t, mine_t = near.at[turn], four.at[turn], far.at[turn], swap.at[turn], mine.at[turn]
        ring_far_t, sum_far_t, cross_t = ring_far.at[turn], sum_far.at[turn], cross.at[turn]
        fin_far_t, all_far_t = fin_far.at[turn], all_far.at[turn]
        near_in_t, ring_four_t, fin_four_t, all_four_t = near_in.at[turn], ring_four.at[turn], fin_four.at[turn], all_four.at[turn]

        far_t[...] = make_far()
        if turn == 0:
            pl.semaphore_wait(barrier, len(peers))
        theirs = pl.ds(pl.multiple_of(32 * (1 - core), 32), 32)
        ours = pl.ds(pl.multiple_of(32 * core, 32), 32)
        core_copy = Group(swap_t)
        core_copy.send(far_t.at[theirs], swap_t, (other, z))
        during_core()
        core_copy.wait_recv()
        mine_t[...] = far_t[ours, :] + swap_t[...]

        far_ring = Group(ring_far_t.at[pl.ds(1, 7)])
        for k in RING:
            dest = (z + k) % 8
            rows = pl.ds(pl.multiple_of(8 * (dest % 4), 8), 8)
            far_ring.send(mine_t.at[rows], ring_far_t.at[k], (wide, dest))

        levels = apart(make_near())
        four_t[...] = levels[3]
        for level in (1, 2, 3):
            near_t[level] = pack(levels[level - 1])
        four_ring = Group(ring_four_t.at[pl.ds(1, 7)])
        for k in RING:
            dest = (z + k) % 8
            rows = pl.ds(pl.multiple_of(16 * (dest % 4), 16), 16)
            four_ring.send(four_t.at[rows], ring_four_t.at[k], (wide, dest))
        near_copies = Group(near_in_t.at[pl.ds(1, 7)])
        for m in NEAR_PEERS:
            near_copies.send(near_t.at[near_level(m)], near_in_t.at[m], (wide, flip(z, m)))

        hidden(0)

        own16 = pl.ds(pl.multiple_of(16 * slot, 16), 16)
        own8 = pl.ds(pl.multiple_of(8 * slot, 8), 8)
        far_ring.wait_recv()
        total = mine_t[own8, :]
        for k in range(1, 8):
            total = total + ring_far_t[k]
        sum_far_t[...] = total

        plane_copies = Group(cross_t)
        for index, (m, tile) in enumerate(CROSS):
            plane_copies.send(sum_far_t.at[:, pl.ds(128 * tile, 128)], cross_t.at[index], (flip(plane, m) * 2 + core, z))

        four_ring.wait_recv()
        total = four_t[own16, :]
        for k in range(1, 8):
            total = total + ring_four_t[k]
        fin_four_t[...] = total
        four_gather = Group(all_four_t)
        for reader in readers + (z,):
            four_gather.send(fin_four_t, all_four_t.at[own16], (other, reader))

        hidden(1)

        plane_copies.wait_recv()
        for tile in range(3):
            lanes = pl.ds(128 * tile, 128)
            value = jnp.zeros((8, 128), F32)
            for level in FAR:
                first, last = tiles_of(level)
                if not first <= tile < last:
                    continue
                part = None
                for m in range(1, 16):
                    if level_of(m) == level:
                        piece = cross_t[CROSS.index((m, tile))]
                        part = piece if part is None else part + piece
                low = FAR_LANE[level] - 128 * tile
                inside = jnp.logical_and(lane >= low, lane < low + RANK)
                value = jnp.where(inside, part, value)
            fin_far_t[:, lanes] = value
        own_far = pl.ds(pl.multiple_of(32 * core + 8 * slot, 8), 8)
        far_gather = Group(all_far_t.at[pl.ds(0, 56)])
        for reader in readers:
            far_gather.send(fin_far_t, all_far_t.at[own_far], (wide, reader))
            far_gather.send(fin_far_t, all_far_t.at[own_far], (other, reader))
        far_gather.send(fin_far_t, all_far_t.at[own_far], (other, z))
        all_far_t[own_far, :] = fin_far_t[...]

        near_copies.wait_recv()
        four_gather.wait_recv()
        c1 = unpack(near_in_t[1])
        c2 = unpack(near_in_t[2] + near_in_t[3])
        c3 = unpack((near_in_t[4] + near_in_t[5]) + (near_in_t[6] + near_in_t[7]))
        settle(0, together(c1, c2, c3, all_four_t[...]))
        far_gather.wait_recv()
        settle(1, all_far_t[...])

    def far_part(stacked):
        return mul_t(stacked, row_h[HALF:, :], row_l[HALF:, :])

    def near_part(stacked):
        return mul_t(stacked, row_h[:HALF, :], row_l[:HALF, :])

    def local_image(stacked):
        coefs = []
        for h in range(2):
            cols = slice(LEAF * h, LEAF * (h + 1))
            coefs.append(stack_split(mul_t(stacked[:, cols], row0_h[:, cols], row0_l[:, cols])))
        parts = []
        for h in range(2):
            cols = slice(LEAF * h, LEAF * (h + 1))
            image = mul(stacked[:, cols], leaf_h[:, cols], leaf_l[:, cols])
            parts.append(image + mul(coefs[1 - h], col0_h[:, cols], col0_l[:, cols]))
        return jnp.concatenate(parts, axis=1)

    def far_image(group, coefs):
        rows = slice(HALF * group, HALF * (group + 1))
        return mul(stack_split(coefs), col_h[rows, :], col_l[rows, :])

    def refine():
        residual_s = stack_split(base[...])
        parts = []
        for h in range(2):
            cols = slice(LEAF * h, LEAF * (h + 1))
            parts.append(sol[:, cols] + mul(residual_s[:, cols], inv_h[:, cols], inv_l[:, cols]))
        return jnp.concatenate(parts, axis=1)

    loads["sol"].wait()
    sol_s = stack_split(sol[...])

    def first_far():
        parts = []
        for h in range(2):
            loads[("far", h)].wait()
            cols = slice(LEAF * h, LEAF * (h + 1))
            split_rows(rowf.at[pl.ds(HALF, HALF)], row_h.at[pl.ds(HALF, HALF)], row_l.at[pl.ds(HALF, HALF)], cols=cols)
            parts.append(mul_t(sol_s[:, cols], row_h[HALF:, cols], row_l[HALF:, cols]))
        return parts[0] + parts[1]

    near_value = []

    def first_during():
        loads["near"].wait()
        split_rows(rowf.at[pl.ds(0, HALF)], row_h.at[pl.ds(0, HALF)], row_l.at[pl.ds(0, HALF)])
        near_value.append(near_part(sol_s))

    def first_hidden(stage):
        if stage == 0:
            for name in ("leaf", "row0", "col0", "inc"):
                loads[name].wait()
            split_rows(leaf, leaf_h, leaf_l)
            split_rows(row0, row0_h, row0_l)
            split_rows(col0, col0_h, col0_l)
            base[...] = inc[...] - local_image(sol_s)
            loads["inv"].wait()
            split_rows(inv, inv_h, inv_l)
            loads["col"].wait()
            split_rows(colf, col_h, col_l)
            for h in range(2):
                for n in range(2):
                    rows = slice(LEAF * h, LEAF * (h + 1))
                    cols = slice(LEAF * h + 256 * n, LEAF * h + 256 * (n + 1))
                    value = jnp.dot(col_h[HALF:, rows], inv_h[:, cols], preferred_element_type=F32)
                    value = value + jnp.dot(col_l[HALF:, rows], inv_h[:, cols], preferred_element_type=F32)
                    value = value + jnp.dot(col_h[HALF:, rows], inv_l[:, cols], preferred_element_type=F32)
                    high, low = split(value)
                    mid_h[:, cols] = high
                    mid_l[:, cols] = low
        else:
            dims = (((1,), (1,)), ((), ()))
            for low, high in ((0, 256), (256, 384)):
                cols = slice(low, high)
                rows = slice(HALF + low, HALF + high)
                value = lax.dot_general(mid_h[...], row_h[rows, :], dims, preferred_element_type=F32)
                value = value + lax.dot_general(mid_l[...], row_h[rows, :], dims, preferred_element_type=F32)
                value = value + lax.dot_general(mid_h[...], row_l[rows, :], dims, preferred_element_type=F32)
                high, low = split(value)
                map_h[:, cols] = high
                map_l[:, cols] = low

    coefs_far = []

    def first_settle(group, coefs):
        if group == 0:
            base[...] = base[...] - far_image(0, coefs)
            ahead[...] = far_part(stack_split(refine()))
        else:
            coefs_far.append(stack_split(coefs))

    exchange(0, first_far, first_during, lambda: near_value[0], first_hidden, first_settle)

    def second_far():
        return ahead[...] - mul(coefs_far[0], map_h[...], map_l[...])

    def second_during():
        base[...] = base[...] - mul(coefs_far[0], col_h[HALF:, :], col_l[HALF:, :])
        refined[...] = refine()

    def second_near():
        return near_part(stack_split(refined[...]))

    def second_hidden(stage):
        if stage == 0:
            out[...] = inc[...] - local_image(stack_split(refined[...]))

    def second_settle(group, coefs):
        out[...] = out[...] - far_image(group, coefs)

    exchange(1, second_far, second_during, second_near, second_hidden, second_settle)

    for group in groups:
        group.wait_send()


def finish(refined, out, refined_hbm, out_hbm, sem):
    copies = [pltpu.make_async_copy(refined, refined_hbm, sem.at[0]), pltpu.make_async_copy(out, out_hbm, sem.at[1])]
    for copy in copies:
        copy.start()
    for copy in copies:
        copy.wait()


def per_device(solution, incident, leaf_blocks, leaf_inverse, col_basis, row_basis):
    vmem = pltpu.VMEM
    scratch = [
        vmem((COLS, ROWS), F32), vmem((COLS, ROWS), F32), vmem((LEAF, ROWS), F32), vmem((LEAF, ROWS), F32),
        vmem((2 * HALF, ROWS), F32), vmem((2 * HALF, ROWS), F32), vmem((RANK, ROWS), F32), vmem((RANK, ROWS), F32),
        vmem((LEAF, ROWS), BF16), vmem((LEAF, ROWS), BF16), vmem((LEAF, ROWS), BF16), vmem((LEAF, ROWS), BF16),
        vmem((2 * HALF, ROWS), BF16), vmem((2 * HALF, ROWS), BF16),
        vmem((2 * HALF, ROWS), BF16), vmem((2 * HALF, ROWS), BF16),
        vmem((RANK, ROWS), BF16), vmem((RANK, ROWS), BF16), vmem((RANK, ROWS), BF16), vmem((RANK, ROWS), BF16),
        vmem((HALF, ROWS), BF16), vmem((HALF, ROWS), BF16),
        vmem((HALF, HALF), BF16), vmem((HALF, HALF), BF16),
        vmem((COLS, ROWS), F32),
        vmem((COLS, HALF), F32),
        vmem((2, 4, 48, 128), F32),
        vmem((2, COLS, 128), F32),
        vmem((2, COLS, HALF), F32),
        vmem((2, 32, HALF), F32),
        vmem((2, 32, HALF), F32),
        vmem((2, 8, 8, HALF), F32),
        vmem((2, 8, HALF), F32),
        vmem((2, len(CROSS), 8, 128), F32),
        vmem((2, 8, HALF), F32),
        vmem((2, COLS, HALF), F32),
        vmem((2, 8, 48, 128), F32),
        vmem((2, 8, 16, 128), F32),
        vmem((2, 16, 128), F32),
        vmem((2, COLS, 128), F32),
        pltpu.SemaphoreType.DMA((10,)),
        pltpu.SemaphoreType.DMA((14,)),
        pltpu.SemaphoreType.DMA((14,)),
    ]
    anywhere = pl.BlockSpec(memory_space=pltpu.HBM)
    resident = pl.BlockSpec(memory_space=pltpu.VMEM)
    shape = jax.ShapeDtypeStruct((COLS, ROWS), F32)
    results = pl.pallas_call(
        kernel,
        out_shape=(shape, shape),
        in_specs=[anywhere] * 6,
        out_specs=(resident, resident),
        scratch_shapes=scratch,
        compiler_params=pltpu.CompilerParams(
            collective_id=0, has_side_effects=True, vmem_limit_bytes=36 * 1024 * 1024),
    )(*(pltpu.with_memory_space_constraint(x, pltpu.HBM) for x in (
        solution, incident, leaf_blocks, leaf_inverse, col_basis, row_basis)))
    return pl.pallas_call(
        finish,
        out_shape=(shape, shape),
        in_specs=[resident, resident],
        out_specs=(anywhere, anywhere),
        scratch_shapes=[pltpu.SemaphoreType.DMA((2,))],
        compiler_params=pltpu.CompilerParams(vmem_limit_bytes=4 * 1024 * 1024),
    )(*results)


def solution(mesh):
    in_specs = (
        P(None, ("wide", "grp")),
        P(None, ("wide", "grp")),
        P(None, ("wide", "grp")),
        P(None, ("wide", "grp")),
        P(None, None, ("wide", "grp")),
        P(None, None, ("wide", "grp")),
    )
    out_specs = (P(None, ("wide", "grp")), P(None, ("wide", "grp")))
    return jax.shard_map(
        per_device, mesh=mesh, in_specs=in_specs, out_specs=out_specs, check_vma=False
    )
```
